32 devices in a mesh: occ: 16 (over z, y, core), vir: 2 (over x).
Axes of the slice: x: 2, y: 2, z: 4, core: 2. Of those that a mesh axis runs over, the one named last changes fastest.
Arguments:
- lambda_triples: bfloat16 [256, 320, 320], P('occ', 'vir'), may hold values from -6 to 6
- amplitude_triples: bfloat16 [256, 320, 320], P('occ', 'vir'), may hold values from -6 to 6
- spin_extent: int32 [256], P('occ'), may hold values from 80 to 320
- ladder_weight: bfloat16 [320, 320], P(None, 'vir'), may hold values from -0.3125 to 0.3125
- cycle_weight: bfloat16 [320, 40], replicated, may hold values from -0.3125 to 0.3125
- lambda_doubles: bfloat16 [40, 320], P(None, 'vir'), may hold values from -1 to 1
Outputs:
- residual: bfloat16 [256, 320, 320], P('occ', 'vir')
The draws below stay inside these ranges and needn't reach their ends.
All inputs are finite; a program needn't handle non-finite values.
Results may differ from the reference program's by a relative error of at most 0.0043.
Values may be sent and summed in bfloat16 or wider, within the bound.
No kernel may reach another device: no remote copies, remote signals or barrier semaphores. Data moves between devices by JAX's collectives and lax.ppermute only.
A program may use at most 64 MiB of HBM per device.

```python
import jax
import jax.numpy as jnp

V = 320
O = 40
TRIPLES = 256


def touch_ends(values, own_key, low, largest):
    dims = values.shape
    place = [jax.random.randint(jax.random.fold_in(own_key, axis), (), 0, dims[axis]) for axis in range(len(dims))]
    values = values.at[tuple(place)].set(low)
    longest = dims.index(max(dims))
    place[longest] = (place[longest] + 1) % dims[longest]
    return values.at[tuple(place)].set(largest)


def steps_of(own_key, dims, pieces, least, high):
    gain = 1.0
    for dim, shards_of in pieces:
        heights = jax.random.uniform(jax.random.fold_in(jax.random.fold_in(own_key, 6), dim), (shards_of,), jnp.float32, least / len(pieces), high / len(pieces))
        gain = gain * jnp.repeat(jnp.exp(heights), dims[dim] // shards_of).reshape((-1,) + (1,) * (len(dims) - 1 - dim))
    return gain


def bell_draw(stream_key, shape, spread, most, split=(), kind=jnp.bfloat16):
    drawn = jax.random.normal(stream_key, shape, jnp.float32) * spread
    if len(split) > 0:
        drawn = steps_of(stream_key, shape, split, -0.22, 0.18) * drawn
    return jnp.clip(drawn, min=-most, max=most).astype(kind)


def setup_inputs(seed: int = 0) -> dict:
    splits = jax.random.split(jax.random.key(seed), 7)
    lambda_triples = bell_draw(splits[0], (TRIPLES, V, V), 1.0, 6.0, ((0, 16), (1, 2)))
    amplitude_triples = bell_draw(splits[1], (TRIPLES, V, V), 1.0, 6.0, ((0, 16), (1, 2)))
    spin_extent = touch_ends(jax.random.randint(splits[2], (TRIPLES,), V // 4, V + 1), jax.random.fold_in(splits[2], 1), V // 4, V).astype(jnp.int32)
    ladder_weight = bell_draw(splits[3], (V, V), V ** -0.5, 0.3125, ((1, 2),))
    cycle_weight = bell_draw(splits[4], (V, O), V ** -0.5, 0.3125)
    lambda_doubles = bell_draw(splits[5], (O, V), O ** -0.5, 1.0, ((1, 2),))
    return {"lambda_triples": lambda_triples, "amplitude_triples": amplitude_triples, "spin_extent": spin_extent, "ladder_weight": ladder_weight, "cycle_weight": cycle_weight, "lambda_doubles": lambda_doubles}


def reference(lambda_triples, amplitude_triples, spin_extent, ladder_weight, cycle_weight, lambda_doubles):
    f32 = jnp.float32
    columns = jnp.arange(V, dtype=jnp.int32)
    keep = columns[None, :] < spin_extent[:, None]
    masked = jnp.where(keep[:, None, :], lambda_triples, jnp.zeros_like(lambda_triples))
    ladder_term = jnp.einsum('tae,eb->tab', masked.astype(f32), ladder_weight.astype(f32))
    cycle_mid = jnp.einsum('tae,em->tam', amplitude_triples.astype(f32), cycle_weight.astype(f32)).astype(jnp.bfloat16)
    cycle_term = jnp.einsum('tam,mb->tab', cycle_mid.astype(f32), lambda_doubles.astype(f32))
    density = jnp.einsum('tae,tbe->ab', masked.astype(f32), amplitude_triples.astype(f32))
    density = (density / jnp.sqrt(f32(TRIPLES * V))).astype(jnp.bfloat16)
    density_term = jnp.einsum('ac,tcb->tab', density.astype(f32), masked.astype(f32)) / jnp.sqrt(f32(V))
    return (ladder_term + cycle_term + density_term).astype(jnp.bfloat16)
```

```python
import functools

import jax
import jax.numpy as jnp
from jax import lax
from jax.experimental import pallas as pl
from jax.experimental.pallas import tpu as pltpu
from jax.sharding import PartitionSpec as P

F32, BF16 = jnp.float32, jnp.bfloat16
NT = (((1,), (1,)), ((), ()))
VMEM = functools.partial(pl.BlockSpec, memory_space=pltpu.VMEM)
SMEM = functools.partial(pl.BlockSpec, memory_space=pltpu.SMEM)
ROWS = (128, 32)


def params(mib, **kw):
    return pltpu.CompilerParams(vmem_limit_bytes=mib << 20, **kw)


def cost(flops, nbytes):
    return pl.CostEstimate(flops=flops, bytes_accessed=nbytes, transcendentals=0)


def keep_row(ext, t, width):
    lane = lax.broadcasted_iota(jnp.int32, (1, width), 1)
    return (lane < ext[t]).astype(F32).astype(BF16)


def pack_kernel(masked, ext, x_ref, o_ref):
    triples, _, width = x_ref.shape
    main = width // 128 * 128
    tail = width - main
    for t in range(0, triples, 2):
        pair = []
        for u in (t, t + 1):
            x = x_ref[u]
            if masked:
                x = x * keep_row(ext, u, width)
            o_ref[:, u * main : (u + 1) * main] = x[:, :main]
            pair.append(x[:, main:])
        at = triples * main + t * tail
        o_ref[:, at : at + 2 * tail] = jnp.concatenate(pair, axis=1)


def pack(x, ext, start, rows, masked):
    triples, _, width = x.shape
    return pl.pallas_call(
        functools.partial(pack_kernel, masked),
        grid=(1,),
        in_specs=[SMEM(), pl.BlockSpec((triples, rows, width), lambda i: (0, start // rows, 0))],
        out_specs=pl.BlockSpec((rows, triples * width), lambda i: (0, 0)),
        out_shape=jax.ShapeDtypeStruct((rows, triples * width), BF16),
        compiler_params=params(16),
        cost_estimate=cost(triples * rows * width * 2, triples * rows * width * 4),
        name="pack",
    )(ext, x)


def gram_kernel(x_ref, y_ref, o_ref):
    o_ref[...] = lax.dot_general(x_ref[...], y_ref[...], NT, preferred_element_type=F32)


def gram(x, y):
    m, n, k = x.shape[0], y.shape[0], x.shape[1]
    return pl.pallas_call(
        gram_kernel,
        in_specs=[VMEM(), VMEM()],
        out_specs=VMEM(),
        out_shape=jax.ShapeDtypeStruct((m, n), F32),
        compiler_params=params(16),
        cost_estimate=cost(2 * m * n * k, 2 * (m + n) * k),
        name="gram",
    )(x, y)


def base_kernel(step, scale, ext, lam_ref, amp_ref, cyc_ref, wl_ref, den_ref, o_ref):
    i = pl.program_id(0)
    width = lam_ref.shape[2]
    main = width // 128 * 128
    tail = width - main
    den = den_ref[...]
    for u in range(step):
        t = i * step + u
        lam = lam_ref[u] * keep_row(ext, t, width)
        mid = lax.dot_general(amp_ref[u], cyc_ref[...], NT, preferred_element_type=F32).astype(BF16)
        both = jnp.concatenate([lam, mid], axis=1)
        near = lax.dot_general(both, wl_ref[...], NT, preferred_element_type=F32)
        o_ref[u] = near + jnp.dot(den, lam, preferred_element_type=F32) * scale


def base(lam, amp, ext, cyc, wl, den, scale, step=4):
    triples, rows, width = lam.shape
    block = pl.BlockSpec((step, rows, width), lambda i: (i, 0, 0))
    whole = lambda x: pl.BlockSpec(x.shape, lambda i: (0, 0))
    return pl.pallas_call(
        functools.partial(base_kernel, step, scale),
        grid=(triples // step,),
        in_specs=[SMEM(), block, block, whole(cyc), whole(wl), whole(den)],
        out_specs=block,
        out_shape=jax.ShapeDtypeStruct(lam.shape, F32),
        compiler_params=params(24),
        cost_estimate=cost(2 * triples * rows * width * (width + 64 + rows), triples * rows * width * 8),
        name="near",
    )(ext, lam, amp, cyc, wl, den)


def last_kernel(scale, den_ref, *refs):
    *got, base_ref, _, o_ref = refs
    triples, rows, width = base_ref.shape
    main = width // 128 * 128
    tail = width - main
    den = den_ref[...]

    def product(lo, size):
        total, at = None, 0
        for g in got:
            k = g.shape[0]
            part = jnp.dot(den[:, at : at + k], g[:, lo : lo + size], preferred_element_type=F32)
            total = part if total is None else total + part
            at += k
        return total * scale

    for t in range(0, triples, 2):
        ends = product(triples * main + t * tail, 2 * tail)
        for u in (t, t + 1):
            s = (u - t) * tail
            o_ref[u, :, :main] = (base_ref[u, :, :main] + product(u * main, main)).astype(BF16)
            o_ref[u, :, main:] = (base_ref[u, :, main:] + ends[:, s : s + tail]).astype(BF16)


def last(den, got, near, out, start, scale):
    triples, _, width = near.shape
    rows = den.shape[0]
    block = pl.BlockSpec((triples, rows, width), lambda i: (0, start // rows, 0))
    whole = lambda x: pl.BlockSpec(x.shape, lambda i: (0, 0))
    if out is None:
        out, spec, alias = jnp.zeros((8, 128), BF16), pl.BlockSpec((8, 128), lambda i: (0, 0)), {}
    else:
        spec, alias = pl.BlockSpec(memory_space=pl.ANY), {len(got) + 2: 0}
    return pl.pallas_call(
        functools.partial(last_kernel, scale),
        grid=(1,),
        in_specs=[whole(den), *map(whole, got), block, spec],
        out_specs=block,
        out_shape=jax.ShapeDtypeStruct(near.shape, BF16),
        input_output_aliases=alias,
        compiler_params=params(32),
        cost_estimate=cost(2 * triples * rows * width * 160, triples * rows * width * 6),
        name="last",
    )(den, *got, near, out)


def permute(x, flip, swap=0):
    n, v = lax.axis_size("occ"), lax.axis_size("vir")
    if not swap:
        return lax.ppermute(x, "occ", [(i, i ^ flip) for i in range(n)])
    return lax.ppermute(x, ("occ", "vir"), [(i * v + j, (i ^ flip) * v + (j ^ swap)) for i in range(n) for j in range(v)])


def total_of(x, swap):
    n = lax.axis_size("occ")
    x = x + permute(x, 1)
    if swap:
        x = permute(x, 0, 1) + permute(x, 2, 1)
    else:
        x = x + permute(x, 2)
    bit = 4
    while bit < n:
        if 2 * bit < n:
            x = (x + permute(x, bit)) + (permute(x, 2 * bit) + permute(x, 3 * bit))
            bit *= 4
        else:
            x = x + permute(x, bit)
            bit *= 2
    return x


def on_device(lam, amp, ext, ladder, cycle, doubles):
    triples, rows, width = lam.shape
    all_triples = triples * lax.axis_size("occ")
    norm = jnp.sqrt(F32(all_triples * width))
    scale = 1.0 / float(width) ** 0.5
    vir = lax.axis_index("vir")

    starts = [sum(ROWS[:k]) for k in range(len(ROWS))]
    own = [pack(lam, ext, s, r, True) for s, r in zip(starts, ROWS)]
    got = [permute(x, 0, 1) for x in own]

    pad = jnp.zeros((rows, 128 - width % 128 - doubles.shape[0]), BF16)
    wl_own = jnp.concatenate([ladder.T, doubles.T, pad], axis=1)
    wl_got = permute(wl_own, 0, 1)
    wl = jnp.where(vir == 0, jnp.concatenate([wl_own, wl_got]), jnp.concatenate([wl_got, wl_own]))
    cyc = jnp.pad(cycle.T, ((0, 64 - cycle.shape[1]), (0, 0)))

    amp_all = pack(amp, ext, 0, rows, False)
    own_part = jnp.concatenate([gram(x, amp_all) for x in own])
    own_den = (total_of(own_part, 0) / norm).astype(BF16)
    near = base(lam, amp, ext, cyc, wl, own_den, scale)

    out = None
    for g, s in zip(got, starts):
        den = (total_of(gram(g, amp_all), 1) / norm).astype(BF16)
        out = last(den, got, near, out, s, scale)
    return out


def solution(mesh):
    return jax.shard_map(
        on_device,
        mesh=mesh,
        in_specs=(
            P("occ", "vir", None),
            P("occ", "vir", None),
            P("occ"),
            P(None, "vir"),
            P(),
            P(None, "vir"),
        ),
        out_specs=P("occ", "vir", None),
        check_vma=False,
    )
```

```python
import functools

import jax
import jax.numpy as jnp
from jax import lax
from jax.experimental import pallas as pl
from jax.experimental.pallas import tpu as pltpu
from jax.sharding import PartitionSpec as P

F32, BF16 = jnp.float32, jnp.bfloat16
NT = (((1,), (1,)), ((), ()))
VMEM = functools.partial(pl.BlockSpec, memory_space=pltpu.VMEM)
SMEM = functools.partial(pl.BlockSpec, memory_space=pltpu.SMEM)
LATE = 64
EXTRA = 8


def params(mib, **kw):
    return pltpu.CompilerParams(vmem_limit_bytes=mib << 20, **kw)


def cost(flops, nbytes):
    return pl.CostEstimate(flops=flops, bytes_accessed=nbytes, transcendentals=0)


def whole(x):
    return pl.BlockSpec(x.shape, lambda i: (0,) * x.ndim)


def after(x, *others):
    return lax.optimization_barrier((x, *others))[0]


def pack_into(o_ref, x_ref, keep_ref=None):
    triples, _, width = x_ref.shape
    main = width // 128 * 128
    tail = width - main
    for t in range(0, triples, 2):
        pair = []
        for u in (t, t + 1):
            x = x_ref[u]
            if keep_ref is not None:
                x = x * keep_ref[u : u + 1, :].astype(BF16)
            o_ref[:, u * main : (u + 1) * main] = x[:, :main]
            pair.append(x[:, main:])
        at = triples * main + t * tail
        o_ref[:, at : at + 2 * tail] = jnp.concatenate(pair, axis=1)


def core_of():
    return lax.rem(lax.axis_index("occ"), 2)


def spread(x):
    return jnp.concatenate([x[i : i + EXTRA] for i in range(0, x.shape[0], EXTRA)], axis=1)


def gather_back(x, width):
    return jnp.concatenate([x[:, i : i + width] for i in range(0, x.shape[1], width)], axis=0)


def pack_kernel(x_ref, ladder_ref, doubles_ref, o_ref):
    rows = x_ref.shape[1]
    pack_into(o_ref.at[:rows], x_ref)
    half = ladder_ref.shape[0] // 2
    start = pl.multiple_of(core_of() * half, 16)
    parts = [spread(ladder_ref[pl.ds(start, half), :].astype(F32)), spread(doubles_ref[...].astype(F32))]
    used = sum(p.shape[1] for p in parts)
    parts.append(jnp.zeros((EXTRA, o_ref.shape[1] - used), F32))
    o_ref[rows:, :] = jnp.concatenate(parts, axis=1).astype(BF16)


def pack(x, ladder, doubles, start):
    triples, rows, width = x.shape
    rows = rows - start
    return pl.pallas_call(
        pack_kernel,
        grid=(1,),
        in_specs=[
            pl.BlockSpec((pl.Element(triples), pl.Element(rows), pl.Element(width)), lambda i: (0, start, 0)),
            whole(ladder),
            whole(doubles),
        ],
        out_specs=pl.BlockSpec((rows + EXTRA, triples * width), lambda i: (0, 0)),
        out_shape=jax.ShapeDtypeStruct((rows + EXTRA, triples * width), BF16),
        compiler_params=params(8),
        cost_estimate=cost(triples * rows * width * 2, triples * rows * width * 4),
        name="pack",
    )(x, ladder, doubles)


def fold(x):
    m = x.shape[0] // 4
    return jnp.concatenate([x[q * m : (q + 1) * m] for q in range(4)], axis=1)


def unfold(x):
    n = x.shape[1] // 4
    return jnp.concatenate([x[:, q * n : (q + 1) * n] for q in range(4)], axis=0)


def product_of(x, y):
    return lax.dot_general(x, y, NT, preferred_element_type=F32)


def prepare_kernel(lam_ref, early_ref, amp_ref, keep_ref, late_ref, all_ref, o_ref):
    pack_into(late_ref, lam_ref)
    pack_into(all_ref, amp_ref, keep_ref)
    y = all_ref[...]
    o_ref[...] = fold(jnp.concatenate([product_of(late_ref[...], y), product_of(early_ref[: y.shape[0] - LATE], y)]))


def prepare(lam, early, amp, keep):
    triples, rows, width = lam.shape
    size = triples * width
    return pl.pallas_call(
        prepare_kernel,
        grid=(1,),
        in_specs=[pl.BlockSpec((triples, LATE, width), lambda i: (0, 0, 0)), whole(early), whole(amp), whole(keep)],
        out_specs=[pl.BlockSpec(s, lambda i: (0, 0)) for s in ((LATE, size), (rows, size), (rows // 4, 4 * rows))],
        out_shape=[
            jax.ShapeDtypeStruct((LATE, size), BF16),
            jax.ShapeDtypeStruct((rows, size), BF16),
            jax.ShapeDtypeStruct((rows // 4, 4 * rows), F32),
        ],
        compiler_params=params(18),
        cost_estimate=cost(2 * rows * rows * size, 6 * rows * size),
        name="prepare",
    )(lam, early, amp, keep)


def gram_kernel(m, x_ref, y_ref, o_ref):
    o_ref[...] = fold(product_of(x_ref[:m], y_ref[...]))


def gram(x, y, m):
    n, k = y.shape
    return pl.pallas_call(
        functools.partial(gram_kernel, m),
        in_specs=[VMEM(), VMEM()],
        out_specs=VMEM(),
        out_shape=jax.ShapeDtypeStruct((m // 4, 4 * n), F32),
        compiler_params=params(8),
        cost_estimate=cost(2 * m * n * k, 2 * (m + n) * k),
        name="gram",
    )(x, y)


def near_kernel(
    step, norm, scale, keep_ref, lam_ref, amp_ref, cyc_ref, ladder_ref, doubles_ref, mine_ref, other_ref, den_ref, o_ref, w_ref, d_ref
):
    i = pl.program_id(0)
    half, width = ladder_ref.shape

    @pl.when(i == 0)
    def _():
        core, vir = core_of(), lax.axis_index("vir")
        size = half // 2 // EXTRA * width
        mine, other = mine_ref[...].astype(F32), other_ref[...].astype(F32)
        w_ref[pl.ds(pl.multiple_of(vir * half, 16), half), :] = ladder_ref[...]
        there = (1 - vir) * half
        for x, c in ((mine, core), (other, 1 - core)):
            at = pl.multiple_of(there + c * (half // 2), 16)
            w_ref[pl.ds(at, half // 2), :] = gather_back(x[:, :size], width).astype(BF16)
        own = doubles_ref[...].astype(F32)
        got = gather_back(mine[:, size : size + own.shape[0] // EXTRA * half], half)
        first = vir == 0
        d_ref[:, :half] = jnp.where(first, own, got).astype(BF16)
        d_ref[:, half:] = jnp.where(first, got, own).astype(BF16)

    den = (unfold(den_ref[...]) / norm).astype(BF16)
    for u in range(step):
        lam = lam_ref[u] * keep_ref[pl.ds(i * step + u, 1), :].astype(BF16)
        mid = product_of(amp_ref[u], cyc_ref[...]).astype(BF16)
        near = product_of(lam, w_ref[...]) + jnp.dot(mid, d_ref[...], preferred_element_type=F32)
        o_ref[u] = near + jnp.dot(den, lam, preferred_element_type=F32) * scale


def near_of(lam, amp, keep, cyc, ladder, doubles, mine, other, den, norm, scale, step=4):
    triples, rows, width = lam.shape
    block = pl.BlockSpec((step, rows, width), lambda i: (i, 0, 0))
    return pl.pallas_call(
        functools.partial(near_kernel, step, norm, scale),
        grid=(triples // step,),
        in_specs=[whole(keep), block, block, *map(whole, (cyc, ladder, doubles, mine, other, den))],
        out_specs=block,
        out_shape=jax.ShapeDtypeStruct(lam.shape, F32),
        scratch_shapes=[pltpu.VMEM((width, width), BF16), pltpu.VMEM((doubles.shape[0], width), BF16)],
        compiler_params=params(10),
        cost_estimate=cost(2 * triples * rows * width * (width + 64 + rows), triples * rows * width * 8),
        name="near",
    )(keep, lam, amp, cyc, ladder, doubles, mine, other, den)


def last_kernel(order, norm, scale, keep_ref, den_ref, *refs):
    *got, near_ref, _, o_ref = refs
    triples, rows, width = near_ref.shape
    got = [g[:n] for n, g in zip((LATE, den_ref.shape[1] // 4 - LATE), got)]
    main = width // 128 * 128
    tail = width - main
    den = unfold(den_ref[...].astype(F32))
    if norm is not None:
        den = den / norm
    den = den.astype(BF16)
    den = jnp.concatenate([den[:, s : s + g.shape[0]] for s, g in zip(order, got)], axis=1)
    all_got = jnp.concatenate(got, axis=0)

    def product(lo, size):
        return jnp.dot(den, all_got[:, lo : lo + size], preferred_element_type=F32) * scale

    for t in range(0, triples, 2):
        ends = product(triples * main + t * tail, 2 * tail)
        for u in (t, t + 1):
            s = (u - t) * tail
            keep = keep_ref[u : u + 1, :]
            o_ref[u, :, :main] = (near_ref[u, :, :main] + product(u * main, main) * keep[:, :main]).astype(BF16)
            o_ref[u, :, main:] = (near_ref[u, :, main:] + ends[:, s : s + tail] * keep[:, main:]).astype(BF16)


def last(keep, den, got, order, near, out, start, rows, norm, scale):
    triples, _, width = near.shape
    spec = pl.BlockSpec((pl.Element(triples), pl.Element(rows), pl.Element(width)), lambda i: (0, start, 0))
    if out is None:
        out, alias = jnp.zeros((8, 128), BF16), {}
    else:
        alias = {len(got) + 3: 0}
    return pl.pallas_call(
        functools.partial(last_kernel, order, norm, scale),
        in_specs=[whole(keep), whole(den), *map(whole, got), spec, pl.BlockSpec(memory_space=pl.ANY)],
        grid=(1,),
        out_specs=spec,
        out_shape=jax.ShapeDtypeStruct(near.shape, BF16),
        input_output_aliases=alias,
        compiler_params=params(14),
        cost_estimate=cost(2 * triples * rows * width * 160, triples * rows * width * 6),
        name="last",
    )(keep, den, *got, near, out)


def permute(x, flip, swap=0):
    n, v = lax.axis_size("occ"), lax.axis_size("vir")
    if not swap:
        return lax.ppermute(x, "occ", [(i, i ^ flip) for i in range(n)])
    return lax.ppermute(x, ("occ", "vir"), [(i * v + j, (i ^ flip) * v + (j ^ swap)) for i in range(n) for j in range(v)])


def far_sum(x):
    n = lax.axis_size("occ")
    bit = 4
    while bit < n:
        if 2 * bit < n:
            x = (x + permute(x, bit)) + (permute(x, 2 * bit) + permute(x, 3 * bit))
            bit *= 4
        else:
            x = x + permute(x, bit)
            bit *= 2
    return x


def near_sum(x):
    return (x + permute(x, 1)) + (permute(x, 2) + permute(x, 3))


def crossed_sum(x):
    x = x + permute(x, 1)
    return permute(x, 0, 1) + permute(x, 2, 1)


def on_device(lam, amp, ext, ladder, cycle, doubles):
    triples, rows, width = lam.shape
    all_triples = triples * lax.axis_size("occ")
    norm = float(all_triples * width) ** 0.5
    scale = 1.0 / float(width) ** 0.5
    early_rows = rows - LATE

    early_own = pack(lam, ladder.T, doubles, LATE)
    early_got = permute(early_own, 0, 1)
    keep = (lax.broadcasted_iota(jnp.int32, (triples, width), 1) < ext[:, None]).astype(F32)
    late_own, amp_all, own_den = prepare(lam, early_own, amp, keep)
    late_got = permute(late_own, 0, 1)

    own_den = near_sum(own_den)
    early_got = after(early_got, own_den)
    own_den = far_sum(own_den)

    early = near_sum(gram(early_got, amp_all, early_rows))
    mine = early_got[early_rows:]
    other = permute(mine, 1)
    near = near_of(lam, amp, keep, cycle.T, ladder.T, doubles, mine, other, after(own_den, early), norm, scale)

    early = far_sum(early)
    late_got = after(late_got, near)
    early = permute((early / norm).astype(BF16), 0, 1)
    late = crossed_sum(gram(late_got, amp_all, LATE))
    early = after(early, late)
    late = far_sum(late)

    order = (0, LATE)
    got = (late_got, early_got)
    out = last(keep, early, got, order, near, None, LATE, early_rows, None, scale)
    return last(keep, late, got, order, near, out, 0, LATE, norm, scale)


def solution(mesh):
    return jax.shard_map(
        on_device,
        mesh=mesh,
        in_specs=(
            P("occ", "vir", None),
            P("occ", "vir", None),
            P("occ"),
            P(None, "vir"),
            P(),
            P(None, "vir"),
        ),
        out_specs=P("occ", "vir", None),
        check_vma=False,
    )
```

```python
import functools

import jax
import jax.numpy as jnp
from jax import lax
from jax.experimental import pallas as pl
from jax.experimental.pallas import tpu as pltpu
from jax.sharding import PartitionSpec as P

F32, BF16 = jnp.float32, jnp.bfloat16
NT = (((1,), (1,)), ((), ()))
VMEM = functools.partial(pl.BlockSpec, memory_space=pltpu.VMEM)
SMEM = functools.partial(pl.BlockSpec, memory_space=pltpu.SMEM)
LATE = 64
FIRST = 32
PARTS = 4
EXTRA = 8


def params(mib, **kw):
    return pltpu.CompilerParams(vmem_limit_bytes=mib << 20, **kw)


def cost(flops, nbytes):
    return pl.CostEstimate(flops=flops, bytes_accessed=nbytes, transcendentals=0)


def whole(x):
    return pl.BlockSpec(x.shape, lambda i: (0,) * x.ndim)


def after(x, *others):
    return lax.optimization_barrier((x, *others))[0]


def pack_into(o_ref, x_ref, keep_ref=None):
    triples, _, width = x_ref.shape
    main = width // 128 * 128
    tail = width - main
    for t in range(0, triples, 2):
        pair = []
        for u in (t, t + 1):
            x = x_ref[u]
            if keep_ref is not None:
                x = x * keep_ref[u : u + 1, :].astype(BF16)
            o_ref[:, u * main : (u + 1) * main] = x[:, :main]
            pair.append(x[:, main:])
        at = triples * main + t * tail
        o_ref[:, at : at + 2 * tail] = jnp.concatenate(pair, axis=1)


def core_of():
    return lax.rem(lax.axis_index("occ"), 2)


def spread(x):
    return jnp.concatenate([x[i : i + EXTRA] for i in range(0, x.shape[0], EXTRA)], axis=1)


def gather_back(x, width):
    return jnp.concatenate([x[:, i : i + width] for i in range(0, x.shape[1], width)], axis=0)


def pack_kernel(start, x_ref, ladder_ref, doubles_ref, o_ref, p_ref, x_buf, l_buf, d_buf, sems):
    triples, rows, _ = x_buf.shape
    half = ladder_ref.shape[0] // 2
    n = triples // PARTS
    first = pl.multiple_of(core_of() * half, 16)
    copies = [(x_ref.at[pl.ds(k * n, n), pl.ds(start, rows)], x_buf.at[pl.ds(k * n, n)]) for k in range(PARTS)]
    copies += [(ladder_ref.at[pl.ds(first, half)], l_buf), (doubles_ref, d_buf)]
    copies = [pltpu.make_async_copy(src, dst, sems.at[k]) for k, (src, dst) in enumerate(copies)]
    for c in copies:
        c.start()
    for c in copies:
        c.wait()
    pack_into(o_ref.at[:FIRST], x_buf.at[:, :FIRST])
    pack_into(p_ref, x_buf.at[:, FIRST:])
    parts = [spread(l_buf[...].astype(F32)), spread(d_buf[...].astype(F32))]
    used = sum(p.shape[1] for p in parts)
    parts.append(jnp.zeros((EXTRA, o_ref.shape[1] - used), F32))
    o_ref[FIRST:, :] = jnp.concatenate(parts, axis=1).astype(BF16)


def pack(x, ladder, doubles, start):
    triples, rows, width = x.shape
    rows = rows - start
    shapes = [(FIRST + EXTRA, triples * width), (rows - FIRST, triples * width)]
    return pl.pallas_call(
        functools.partial(pack_kernel, start),
        in_specs=[pl.BlockSpec(memory_space=pltpu.HBM)] * 3,
        out_specs=[VMEM()] * 2,
        out_shape=[jax.ShapeDtypeStruct(s, BF16) for s in shapes],
        scratch_shapes=[
            pltpu.VMEM((triples, rows, width), BF16),
            pltpu.VMEM((ladder.shape[0] // 2, width), BF16),
            pltpu.VMEM(doubles.shape, BF16),
            pltpu.SemaphoreType.DMA((PARTS + 2,)),
        ],
        compiler_params=params(8),
        cost_estimate=cost(triples * rows * width * 2, triples * rows * width * 4),
        name="pack",
    )(*(pltpu.with_memory_space_constraint(y, pltpu.HBM) for y in (x, ladder, doubles)))


def fold_of(rows):
    return 5 if rows % 80 == 0 and rows < 160 else 4


def fold(x):
    q = fold_of(x.shape[0])
    m = x.shape[0] // q
    return jnp.concatenate([x[k * m : (k + 1) * m] for k in range(q)], axis=1)


def unfold(x, n):
    return jnp.concatenate([x[:, k : k + n] for k in range(0, x.shape[1], n)], axis=0)


def folded(m, n):
    q = fold_of(m)
    return jax.ShapeDtypeStruct((m // q, q * n), F32)


def product_of(x, y):
    return lax.dot_general(x, y, NT, preferred_element_type=F32)


def prepare_kernel(lam_ref, first_ref, early_ref, amp_ref, keep_ref, late_ref, all_ref, o_ref):
    pack_into(late_ref, lam_ref)
    pack_into(all_ref, amp_ref, keep_ref)
    y = all_ref[...]
    o_ref[...] = fold(jnp.concatenate([product_of(x, y) for x in (late_ref[...], first_ref[:FIRST], early_ref[...])]))


def prepare(lam, first, early, amp, keep):
    triples, rows, width = lam.shape
    size = triples * width
    return pl.pallas_call(
        prepare_kernel,
        grid=(1,),
        in_specs=[pl.BlockSpec((triples, LATE, width), lambda i: (0, 0, 0)), whole(first), whole(early), whole(amp), whole(keep)],
        out_specs=[pl.BlockSpec(s, lambda i: (0, 0)) for s in ((LATE, size), (rows, size), (rows // 4, 4 * rows))],
        out_shape=[
            jax.ShapeDtypeStruct((LATE, size), BF16),
            jax.ShapeDtypeStruct((rows, size), BF16),
            jax.ShapeDtypeStruct((rows // 4, 4 * rows), F32),
        ],
        compiler_params=params(18),
        cost_estimate=cost(2 * rows * rows * size, 6 * rows * size),
        name="prepare",
    )(lam, first, early, amp, keep)


def gram_kernel(*refs):
    *xs, y_ref, o_ref = refs
    y = y_ref[...]
    o_ref[...] = fold(jnp.concatenate([product_of(x[: x.shape[0] // 16 * 16], y) for x in xs]))


def gram(xs, y):
    m, (n, k) = sum(x.shape[0] // 16 * 16 for x in xs), y.shape
    return pl.pallas_call(
        gram_kernel,
        in_specs=[VMEM()] * (len(xs) + 1),
        out_specs=VMEM(),
        out_shape=folded(m, n),
        compiler_params=params(8),
        cost_estimate=cost(2 * m * n * k, 2 * (m + n) * k),
        name="gram",
    )(*xs, y)


def near_kernel(step, keep_ref, lam_ref, amp_ref, cyc_ref, ladder_ref, doubles_ref, mine_ref, other_ref, o_ref, w_ref, d_ref):
    i = pl.program_id(0)
    half, width = ladder_ref.shape
    rows = lam_ref.shape[1]

    @pl.when(i == 0)
    def _():
        core, vir = core_of(), lax.axis_index("vir")
        size = half // 2 // EXTRA * width
        mine, other = mine_ref[...].astype(F32), other_ref[...].astype(F32)
        w_ref[pl.ds(pl.multiple_of(vir * half, 16), half), :] = ladder_ref[...]
        there = (1 - vir) * half
        for x, c in ((mine, core), (other, 1 - core)):
            at = pl.multiple_of(there + c * (half // 2), 16)
            w_ref[pl.ds(at, half // 2), :] = gather_back(x[:, :size], width).astype(BF16)
        own = doubles_ref[...].astype(F32)
        got = gather_back(mine[:, size : size + own.shape[0] // EXTRA * half], half)
        d_ref[:, :half] = jnp.where(vir == 0, own, got).astype(BF16)
        d_ref[:, half:] = jnp.where(vir == 0, got, own).astype(BF16)

    keep = [keep_ref[pl.ds(i * step + u, 1), :].astype(BF16) for u in range(step)]
    lam = jnp.concatenate([lam_ref[u] * keep[u] for u in range(step)], axis=0)
    mid = product_of(amp_ref[...].reshape(step * rows, width), cyc_ref[...]).astype(BF16)
    near = product_of(lam, w_ref[...]) + jnp.dot(mid, d_ref[...], preferred_element_type=F32)
    o_ref[...] = near.reshape(step, rows, width)


def near_of(lam, amp, keep, cyc, ladder, doubles, mine, other, step=4):
    triples, rows, width = lam.shape
    block = pl.BlockSpec((step, rows, width), lambda i: (i, 0, 0))
    return pl.pallas_call(
        functools.partial(near_kernel, step),
        grid=(triples // step,),
        in_specs=[whole(keep), block, block, *map(whole, (cyc, ladder, doubles, mine, other))],
        out_specs=block,
        out_shape=jax.ShapeDtypeStruct(lam.shape, F32),
        scratch_shapes=[pltpu.VMEM((width, width), BF16), pltpu.VMEM((doubles.shape[0], width), BF16)],
        compiler_params=params(12),
        cost_estimate=cost(2 * triples * rows * width * (width + 64), triples * rows * width * 8),
        name="near",
    )(keep, lam, amp, cyc, ladder, doubles, mine, other)


def add_kernel(step, norm, scale, keep_ref, lam_ref, near_ref, den_ref, o_ref):
    i = pl.program_id(0)
    den = (unfold(den_ref[...], near_ref.shape[1]) / norm).astype(BF16)
    for u in range(step):
        keep = keep_ref[pl.ds(i * step + u, 1), :] * scale
        o_ref[u] = near_ref[u] + jnp.dot(den, lam_ref[u], preferred_element_type=F32) * keep


def add_own(keep, lam, near, den, norm, scale, step=4):
    triples, rows, width = lam.shape
    block = pl.BlockSpec((step, rows, width), lambda i: (i, 0, 0))
    return pl.pallas_call(
        functools.partial(add_kernel, step, norm, scale),
        grid=(triples // step,),
        in_specs=[whole(keep), block, block, whole(den)],
        out_specs=block,
        out_shape=jax.ShapeDtypeStruct(lam.shape, F32),
        input_output_aliases={2: 0},
        compiler_params=params(12),
        cost_estimate=cost(2 * triples * rows * width * rows, triples * rows * width * 10),
        name="add_own",
    )(keep, lam, near, den)


def last_kernel(norm, scale, keep_ref, den_ref, *refs):
    *got, near_ref, _, o_ref = refs
    triples, rows, width = near_ref.shape
    main = width // 128 * 128
    tail = width - main
    den = unfold(den_ref[...].astype(F32), sum(g.shape[0] // 16 * 16 for g in got))
    if norm is not None:
        den = den / norm
    den = den.astype(BF16)
    all_got = jnp.concatenate([g[: g.shape[0] // 16 * 16] for g in got], axis=0)

    def product(lo, size):
        return jnp.dot(den, all_got[:, lo : lo + size], preferred_element_type=F32) * scale

    for t in range(0, triples, 2):
        ends = product(triples * main + t * tail, 2 * tail)
        for u in (t, t + 1):
            s = (u - t) * tail
            keep = keep_ref[u : u + 1, :]
            o_ref[u, :, :main] = (near_ref[u, :, :main] + product(u * main, main) * keep[:, :main]).astype(BF16)
            o_ref[u, :, main:] = (near_ref[u, :, main:] + ends[:, s : s + tail] * keep[:, main:]).astype(BF16)


def last(keep, den, got, near, out, start, rows, norm, scale):
    triples, _, width = near.shape
    spec = pl.BlockSpec((pl.Element(triples), pl.Element(rows), pl.Element(width)), lambda i: (0, start, 0))
    if out is None:
        out, alias = jnp.zeros((8, 128), BF16), {}
    else:
        alias = {len(got) + 3: 0}
    return pl.pallas_call(
        functools.partial(last_kernel, norm, scale),
        in_specs=[whole(keep), whole(den), *map(whole, got), spec, pl.BlockSpec(memory_space=pl.ANY)],
        grid=(1,),
        out_specs=spec,
        out_shape=jax.ShapeDtypeStruct(near.shape, BF16),
        input_output_aliases=alias,
        compiler_params=params(14),
        cost_estimate=cost(2 * triples * rows * width * 160, triples * rows * width * 6),
        name="last",
    )(keep, den, *got, near, out)


def permute(x, flip, swap=0):
    n, v = lax.axis_size("occ"), lax.axis_size("vir")
    if not swap:
        return lax.ppermute(x, "occ", [(i, i ^ flip) for i in range(n)])
    return lax.ppermute(x, ("occ", "vir"), [(i * v + j, (i ^ flip) * v + (j ^ swap)) for i in range(n) for j in range(v)])


def far_sum(x):
    n = lax.axis_size("occ")
    bit = 4
    while bit < n:
        if 2 * bit < n:
            far, mid, close = permute(x, 3 * bit), permute(x, 2 * bit), permute(x, bit)
            x = (x + close) + (mid + far)
            bit *= 4
        else:
            x = x + permute(x, bit)
            bit *= 2
    return x


def near_sum(x):
    far, mid, close = permute(x, 3), permute(x, 2), permute(x, 1)
    return (x + close) + (mid + far)


def crossed_sum(x):
    x = x + permute(x, 1)
    far, close = permute(x, 2, 1), permute(x, 0, 1)
    return close + far


def on_device(lam, amp, ext, ladder, cycle, doubles):
    triples, rows, width = lam.shape
    all_triples = triples * lax.axis_size("occ")
    norm = float(all_triples * width) ** 0.5
    scale = 1.0 / float(width) ** 0.5
    early_rows = rows - LATE

    ladder = ladder.T
    first_own, early_own = pack(lam, ladder, doubles, LATE)
    first_got, early_got = permute(first_own, 0, 1), permute(early_own, 0, 1)
    keep = (lax.broadcasted_iota(jnp.int32, (triples, width), 1) < ext[:, None]).astype(F32)
    late_own, amp_all, own_den = prepare(lam, first_own, early_own, amp, keep)
    late_got = permute(late_own, 0, 1)

    own_den = near_sum(own_den)
    first_got = after(first_got, own_den)
    own_den = far_sum(own_den)
    mine = first_got[FIRST:]
    other = permute(mine, 1)
    near = near_of(lam, amp, keep, cycle.T, ladder, doubles, mine, other)

    early_got = after(early_got, near)
    early = near_sum(gram((first_got, early_got), amp_all))
    near = add_own(keep, lam, near, after(own_den, early), norm, scale)

    early = far_sum(early)
    late_got = after(late_got, near)
    early = permute((early / norm).astype(BF16), 0, 1)
    late = crossed_sum(gram((late_got,), amp_all))
    early = after(early, late)
    late = (far_sum(late) / norm).astype(BF16)

    got = (late_got, first_got, early_got)
    out = last(keep, early, got, near, None, LATE, early_rows, None, scale)
    return last(keep, late, got, near, out, 0, LATE, None, scale)


def solution(mesh):
    return jax.shard_map(
        on_device,
        mesh=mesh,
        in_specs=(
            P("occ", "vir", None),
            P("occ", "vir", None),
            P("occ"),
            P(None, "vir"),
            P(),
            P(None, "vir"),
        ),
        out_specs=P("occ", "vir", None),
        check_vma=False,
    )
```

```python
import functools

import jax
import jax.numpy as jnp
from jax import lax
from jax.experimental import pallas as pl
from jax.experimental.pallas import tpu as pltpu
from jax.sharding import PartitionSpec as P

F32, BF16 = jnp.float32, jnp.bfloat16
NT = (((1,), (1,)), ((), ()))
VMEM = functools.partial(pl.BlockSpec, memory_space=pltpu.VMEM)
SMEM = functools.partial(pl.BlockSpec, memory_space=pltpu.SMEM)
LATE = 64
FIRST = 32
PARTS = 4
EXTRA = 8


def params(mib, **kw):
    return pltpu.CompilerParams(vmem_limit_bytes=mib << 20, **kw)


def cost(flops, nbytes):
    return pl.CostEstimate(flops=flops, bytes_accessed=nbytes, transcendentals=0)


def whole(x):
    return pl.BlockSpec(x.shape, lambda i: (0,) * x.ndim)


def after(x, *others):
    return lax.optimization_barrier((x, *others))[0]


def pack_into(o_ref, x_ref, keep_ref=None):
    triples, _, width = x_ref.shape
    main = width // 128 * 128
    tail = width - main
    for t in range(0, triples, 2):
        pair = []
        for u in (t, t + 1):
            x = x_ref[u]
            if keep_ref is not None:
                x = x * keep_ref[u : u + 1, :].astype(BF16)
            o_ref[:, u * main : (u + 1) * main] = x[:, :main]
            pair.append(x[:, main:])
        at = triples * main + t * tail
        o_ref[:, at : at + 2 * tail] = jnp.concatenate(pair, axis=1)


def core_of():
    return lax.rem(lax.axis_index("occ"), 2)


def spread(x):
    return jnp.concatenate([x[i : i + EXTRA] for i in range(0, x.shape[0], EXTRA)], axis=1)


def gather_back(x, width):
    return jnp.concatenate([x[:, i : i + width] for i in range(0, x.shape[1], width)], axis=0)


def pack_kernel(start, x_ref, ladder_ref, doubles_ref, o_ref, p_ref, x_buf, l_buf, d_buf, sems):
    triples, rows, _ = x_buf.shape
    half = ladder_ref.shape[0] // 2
    n = triples // PARTS
    first = pl.multiple_of(core_of() * half, 16)
    copies = [(x_ref.at[pl.ds(k * n, n), pl.ds(start, rows)], x_buf.at[pl.ds(k * n, n)]) for k in range(PARTS)]
    copies += [(ladder_ref.at[pl.ds(first, half)], l_buf), (doubles_ref, d_buf)]
    copies = [pltpu.make_async_copy(src, dst, sems.at[k]) for k, (src, dst) in enumerate(copies)]
    for c in copies:
        c.start()
    for c in copies:
        c.wait()
    pack_into(o_ref.at[:FIRST], x_buf.at[:, :FIRST])
    pack_into(p_ref, x_buf.at[:, FIRST:])
    parts = [spread(l_buf[...].astype(F32)), spread(d_buf[...].astype(F32))]
    used = sum(p.shape[1] for p in parts)
    parts.append(jnp.zeros((EXTRA, o_ref.shape[1] - used), F32))
    o_ref[FIRST:, :] = jnp.concatenate(parts, axis=1).astype(BF16)


def pack(x, ladder, doubles, start):
    triples, rows, width = x.shape
    rows = rows - start
    shapes = [(FIRST + EXTRA, triples * width), (rows - FIRST, triples * width)]
    return pl.pallas_call(
        functools.partial(pack_kernel, start),
        in_specs=[pl.BlockSpec(memory_space=pltpu.HBM)] * 3,
        out_specs=[VMEM()] * 2,
        out_shape=[jax.ShapeDtypeStruct(s, BF16) for s in shapes],
        scratch_shapes=[
            pltpu.VMEM((triples, rows, width), BF16),
            pltpu.VMEM((ladder.shape[0] // 2, width), BF16),
            pltpu.VMEM(doubles.shape, BF16),
            pltpu.SemaphoreType.DMA((PARTS + 2,)),
        ],
        compiler_params=params(8),
        cost_estimate=cost(triples * rows * width * 2, triples * rows * width * 4),
        name="pack",
    )(*(pltpu.with_memory_space_constraint(y, pltpu.HBM) for y in (x, ladder, doubles)))


def fold_of(rows):
    return 5 if rows % 80 == 0 and rows < 160 else 4


def fold(x):
    q = fold_of(x.shape[0])
    m = x.shape[0] // q
    return jnp.concatenate([x[k * m : (k + 1) * m] for k in range(q)], axis=1)


def unfold(x, n):
    return jnp.concatenate([x[:, k : k + n] for k in range(0, x.shape[1], n)], axis=0)


def folded(m, n):
    q = fold_of(m)
    return jax.ShapeDtypeStruct((m // q, q * n), F32)


def product_of(x, y):
    return lax.dot_general(x, y, NT, preferred_element_type=F32)


def prepare_kernel(lam_ref, first_ref, early_ref, amp_ref, keep_ref, late_ref, all_ref, o_ref):
    pack_into(late_ref, lam_ref)
    pack_into(all_ref, amp_ref, keep_ref)
    y = all_ref[...]
    o_ref[...] = fold(jnp.concatenate([product_of(x, y) for x in (late_ref[...], first_ref[:FIRST], early_ref[...])]))


def prepare(lam, first, early, amp, keep):
    triples, rows, width = lam.shape
    size = triples * width
    return pl.pallas_call(
        prepare_kernel,
        grid=(1,),
        in_specs=[pl.BlockSpec((triples, LATE, width), lambda i: (0, 0, 0)), whole(first), whole(early), whole(amp), whole(keep)],
        out_specs=[pl.BlockSpec(s, lambda i: (0, 0)) for s in ((LATE, size), (rows, size), (rows // 4, 4 * rows))],
        out_shape=[
            jax.ShapeDtypeStruct((LATE, size), BF16),
            jax.ShapeDtypeStruct((rows, size), BF16),
            jax.ShapeDtypeStruct((rows // 4, 4 * rows), F32),
        ],
        compiler_params=params(18),
        cost_estimate=cost(2 * rows * rows * size, 6 * rows * size),
        name="prepare",
    )(lam, first, early, amp, keep)


def gram_kernel(*refs):
    *xs, y_ref, o_ref = refs
    y = y_ref[...]
    o_ref[...] = fold(jnp.concatenate([product_of(x[: x.shape[0] // 16 * 16], y) for x in xs]))


def gram(xs, y):
    m, (n, k) = sum(x.shape[0] // 16 * 16 for x in xs), y.shape
    return pl.pallas_call(
        gram_kernel,
        in_specs=[VMEM()] * (len(xs) + 1),
        out_specs=VMEM(),
        out_shape=folded(m, n),
        compiler_params=params(8),
        cost_estimate=cost(2 * m * n * k, 2 * (m + n) * k),
        name="gram",
    )(*xs, y)


def near_kernel(step, keep_ref, lam_ref, amp_ref, cyc_ref, ladder_ref, doubles_ref, mine_ref, other_ref, o_ref, w_ref, d_ref):
    i = pl.program_id(0)
    half, width = ladder_ref.shape
    rows = lam_ref.shape[1]

    @pl.when(i == 0)
    def _():
        core, vir = core_of(), lax.axis_index("vir")
        size = half // 2 // EXTRA * width
        mine, other = mine_ref[...].astype(F32), other_ref[...].astype(F32)
        w_ref[pl.ds(pl.multiple_of(vir * half, 16), half), :] = ladder_ref[...]
        there = (1 - vir) * half
        for x, c in ((mine, core), (other, 1 - core)):
            at = pl.multiple_of(there + c * (half // 2), 16)
            w_ref[pl.ds(at, half // 2), :] = gather_back(x[:, :size], width).astype(BF16)
        own = doubles_ref[...].astype(F32)
        got = gather_back(mine[:, size : size + own.shape[0] // EXTRA * half], half)
        d_ref[:, :half] = jnp.where(vir == 0, own, got).astype(BF16)
        d_ref[:, half:] = jnp.where(vir == 0, got, own).astype(BF16)

    keep = [keep_ref[pl.ds(i * step + u, 1), :].astype(BF16) for u in range(step)]
    lam = jnp.concatenate([lam_ref[u] * keep[u] for u in range(step)], axis=0)
    mid = product_of(amp_ref[...].reshape(step * rows, width), cyc_ref[...]).astype(BF16)
    near = product_of(lam, w_ref[...]) + jnp.dot(mid, d_ref[...], preferred_element_type=F32)
    o_ref[...] = near.reshape(step, rows, width)


def near_of(lam, amp, keep, cyc, ladder, doubles, mine, other, step=4):
    triples, rows, width = lam.shape
    block = pl.BlockSpec((step, rows, width), lambda i: (i, 0, 0))
    return pl.pallas_call(
        functools.partial(near_kernel, step),
        grid=(triples // step,),
        in_specs=[whole(keep), block, block, *map(whole, (cyc, ladder, doubles, mine, other))],
        out_specs=block,
        out_shape=jax.ShapeDtypeStruct(lam.shape, F32),
        scratch_shapes=[pltpu.VMEM((width, width), BF16), pltpu.VMEM((doubles.shape[0], width), BF16)],
        compiler_params=params(12),
        cost_estimate=cost(2 * triples * rows * width * (width + 64), triples * rows * width * 8),
        name="near",
    )(keep, lam, amp, cyc, ladder, doubles, mine, other)


def add_kernel(step, norm, scale, keep_ref, lam_ref, near_ref, den_ref, o_ref):
    i = pl.program_id(0)
    den = (unfold(den_ref[...], near_ref.shape[1]) / norm).astype(BF16)
    for u in range(step):
        keep = keep_ref[pl.ds(i * step + u, 1), :] * scale
        o_ref[u] = near_ref[u] + jnp.dot(den, lam_ref[u], preferred_element_type=F32) * keep


def add_own(keep, lam, near, den, norm, scale, step=4):
    triples, rows, width = lam.shape
    block = pl.BlockSpec((step, rows, width), lambda i: (i, 0, 0))
    return pl.pallas_call(
        functools.partial(add_kernel, step, norm, scale),
        grid=(triples // step,),
        in_specs=[whole(keep), block, block, whole(den)],
        out_specs=block,
        out_shape=jax.ShapeDtypeStruct(lam.shape, F32),
        input_output_aliases={2: 0},
        compiler_params=params(12),
        cost_estimate=cost(2 * triples * rows * width * rows, triples * rows * width * 10),
        name="add_own",
    )(keep, lam, near, den)


def add_product(o_ref, near_ref, keep_ref, den, got, scale, first):
    triples, _, width = o_ref.shape
    main = width // 128 * 128
    tail = width - main
    ends_at = got.shape[1] - got.shape[1] // width * tail

    def product(lo, size):
        return jnp.dot(den, got[:, lo : lo + size], preferred_element_type=F32) * scale

    for t in range(0, triples, 2):
        ends = product(ends_at + (first + t) * tail, 2 * tail)
        for u in (t, t + 1):
            s = (u - t) * tail
            keep = keep_ref[first + u : first + u + 1, :]
            o_ref[u, :, :main] = (near_ref[u, :, :main] + product((first + u) * main, main) * keep[:, :main]).astype(BF16)
            o_ref[u, :, main:] = (near_ref[u, :, main:] + ends[:, s : s + tail] * keep[:, main:]).astype(BF16)


def early_kernel(scale, keep_ref, den_ref, *refs):
    *got, near_ref, o_ref, all_ref = refs
    at = 0
    for g in got:
        n = g.shape[0] // 16 * 16
        all_ref[at : at + n, :] = g[:n]
        at += n
    den = unfold(den_ref[...].astype(F32), at).astype(BF16)
    add_product(o_ref, near_ref, keep_ref, den, all_ref, scale, 0)


def early_output(keep, den, got, near, start, scale):
    triples, rows, width = near.shape
    spec = pl.BlockSpec((pl.Element(triples), pl.Element(rows - start), pl.Element(width)), lambda i: (0, start, 0))
    all_got = jax.ShapeDtypeStruct((rows, triples * width), BF16)
    return pl.pallas_call(
        functools.partial(early_kernel, scale),
        grid=(1,),
        in_specs=[whole(keep), whole(den), *map(whole, got), spec],
        out_specs=[spec, whole(all_got)],
        out_shape=[jax.ShapeDtypeStruct(near.shape, BF16), all_got],
        compiler_params=params(14),
        cost_estimate=cost(2 * triples * rows * width * 160, triples * rows * width * 6),
        name="early",
    )(keep, den, *got, near)


def late_kernel(scale, keep_ref, den_ref, got_ref, near_ref, _, o_ref, buf, sems):
    triples, rows, _ = buf.shape
    n = triples // PARTS
    den = unfold(den_ref[...].astype(F32), got_ref.shape[0]).astype(BF16)
    copies = []
    for k in range(PARTS):
        part = buf.at[k * n : (k + 1) * n]
        add_product(part, near_ref.at[k * n : (k + 1) * n, :rows], keep_ref, den, got_ref, scale, k * n)
        copies.append(pltpu.make_async_copy(part, o_ref.at[k * n : (k + 1) * n, :rows], sems.at[k]))
        copies[-1].start()
    for c in copies:
        c.wait()


def late_output(keep, den, got, near, out, rows, scale):
    triples, _, width = near.shape
    return pl.pallas_call(
        functools.partial(late_kernel, scale),
        in_specs=[VMEM()] * 4 + [pl.BlockSpec(memory_space=pl.ANY)],
        out_specs=pl.BlockSpec(memory_space=pl.ANY),
        out_shape=jax.ShapeDtypeStruct(near.shape, BF16),
        scratch_shapes=[pltpu.VMEM((triples, rows, width), BF16), pltpu.SemaphoreType.DMA((PARTS,))],
        input_output_aliases={4: 0},
        compiler_params=params(8),
        cost_estimate=cost(2 * triples * rows * width * 160, triples * rows * width * 6),
        name="late",
    )(keep, den, got, near, out)


def permute(x, flip, swap=0):
    n, v = lax.axis_size("occ"), lax.axis_size("vir")
    if not swap:
        return lax.ppermute(x, "occ", [(i, i ^ flip) for i in range(n)])
    return lax.ppermute(x, ("occ", "vir"), [(i * v + j, (i ^ flip) * v + (j ^ swap)) for i in range(n) for j in range(v)])


def far_sum(x):
    n = lax.axis_size("occ")
    bit = 4
    while bit < n:
        if 2 * bit < n:
            far, mid, close = permute(x, 3 * bit), permute(x, 2 * bit), permute(x, bit)
            x = (far + mid) + (close + x)
            bit *= 4
        else:
            x = x + permute(x, bit)
            bit *= 2
    return x


def near_sum(x):
    far, mid, close = permute(x, 3), permute(x, 2), permute(x, 1)
    return (x + close) + (mid + far)


def crossed_sum(x):
    x = x + permute(x, 1)
    far, close = permute(x, 2, 1), permute(x, 0, 1)
    return close + far


def on_device(lam, amp, ext, ladder, cycle, doubles):
    triples, rows, width = lam.shape
    all_triples = triples * lax.axis_size("occ")
    norm = float(all_triples * width) ** 0.5
    scale = 1.0 / float(width) ** 0.5
    early_rows = rows - LATE

    ladder = ladder.T
    first_own, early_own = pack(lam, ladder, doubles, LATE)
    first_got, early_got = permute(first_own, 0, 1), permute(early_own, 0, 1)
    keep = (lax.broadcasted_iota(jnp.int32, (triples, width), 1) < ext[:, None]).astype(F32)
    late_own, amp_all, own_den = prepare(lam, first_own, early_own, amp, keep)
    late_got = permute(late_own, 0, 1)

    own_den = near_sum(own_den)
    first_got = after(first_got, own_den)
    own_den = far_sum(own_den)
    mine = first_got[FIRST:]
    other = permute(mine, 1)
    near = near_of(lam, amp, keep, cycle.T, ladder, doubles, mine, other)

    early_got = after(early_got, near)
    early = near_sum(gram((first_got, early_got), amp_all))
    near = add_own(keep, lam, near, after(own_den, early), norm, scale)

    early = far_sum(early)
    late_got = after(late_got, near)
    early = permute((early / norm).astype(BF16), 0, 1)
    late = crossed_sum(gram((late_got,), amp_all))
    early = after(early, late)
    late = (far_sum(late) / norm).astype(BF16)

    got = (late_got, first_got, early_got)
    out, all_got = early_output(keep, early, got, near, LATE, scale)
    return late_output(keep, late, all_got, near, out, LATE, scale)


def solution(mesh):
    return jax.shard_map(
        on_device,
        mesh=mesh,
        in_specs=(
            P("occ", "vir", None),
            P("occ", "vir", None),
            P("occ"),
            P(None, "vir"),
            P(),
            P(None, "vir"),
        ),
        out_specs=P("occ", "vir", None),
        check_vma=False,
    )
```

```python
import functools

import jax
import jax.numpy as jnp
from jax import lax
from jax.experimental import pallas as pl
from jax.experimental.pallas import tpu as pltpu
from jax.sharding import PartitionSpec as P

F32, BF16 = jnp.float32, jnp.bfloat16
NT = (((1,), (1,)), ((), ()))
VMEM = functools.partial(pl.BlockSpec, memory_space=pltpu.VMEM)
SMEM = functools.partial(pl.BlockSpec, memory_space=pltpu.SMEM)
LATE = 64
FIRST = 48
PARTS = 4
EXTRA = 8


def params(mib, **kw):
    return pltpu.CompilerParams(vmem_limit_bytes=mib << 20, **kw)


def cost(flops, nbytes):
    return pl.CostEstimate(flops=flops, bytes_accessed=nbytes, transcendentals=0)


def whole(x):
    return pl.BlockSpec(x.shape, lambda i: (0,) * x.ndim)


def after(x, *others):
    return lax.optimization_barrier((x, *others))[0]


def pack_into(o_ref, x_ref, keep_ref=None):
    triples, _, width = x_ref.shape
    main = width // 128 * 128
    tail = width - main
    for t in range(0, triples, 2):
        pair = []
        for u in (t, t + 1):
            x = x_ref[u]
            if keep_ref is not None:
                x = x * keep_ref[u : u + 1, :].astype(BF16)
            o_ref[:, u * main : (u + 1) * main] = x[:, :main]
            pair.append(x[:, main:])
        at = triples * main + t * tail
        o_ref[:, at : at + 2 * tail] = jnp.concatenate(pair, axis=1)


def core_of():
    return lax.rem(lax.axis_index("occ"), 2)


def spread(x):
    return jnp.concatenate([x[i : i + EXTRA] for i in range(0, x.shape[0], EXTRA)], axis=1)


def gather_back(x, width):
    return jnp.concatenate([x[:, i : i + width] for i in range(0, x.shape[1], width)], axis=0)


def pack_kernel(start, x_ref, ladder_ref, doubles_ref, o_ref, x_buf, l_buf, d_buf, sems):
    triples, rows, _ = x_buf.shape
    half = ladder_ref.shape[0] // 2
    n = triples // PARTS
    first = pl.multiple_of(core_of() * half, 16)
    copies = [(x_ref.at[pl.ds(k * n, n), pl.ds(start, rows)], x_buf.at[pl.ds(k * n, n)]) for k in range(PARTS)]
    copies += [(ladder_ref.at[pl.ds(first, half)], l_buf), (doubles_ref, d_buf)]
    copies = [pltpu.make_async_copy(src, dst, sems.at[k]) for k, (src, dst) in enumerate(copies)]
    for c in copies:
        c.start()
    for c in copies:
        c.wait()
    pack_into(o_ref.at[:FIRST], x_buf)
    parts = [spread(l_buf[...].astype(F32)), spread(d_buf[...].astype(F32))]
    used = sum(p.shape[1] for p in parts)
    parts.append(jnp.zeros((EXTRA, o_ref.shape[1] - used), F32))
    o_ref[FIRST:, :] = jnp.concatenate(parts, axis=1).astype(BF16)


def pack(x, ladder, doubles, start):
    triples, rows, width = x.shape
    rows = FIRST
    return pl.pallas_call(
        functools.partial(pack_kernel, start),
        in_specs=[pl.BlockSpec(memory_space=pltpu.HBM)] * 3,
        out_specs=VMEM(),
        out_shape=jax.ShapeDtypeStruct((FIRST + EXTRA, triples * width), BF16),
        scratch_shapes=[
            pltpu.VMEM((triples, rows, width), BF16),
            pltpu.VMEM((ladder.shape[0] // 2, width), BF16),
            pltpu.VMEM(doubles.shape, BF16),
            pltpu.SemaphoreType.DMA((PARTS + 2,)),
        ],
        compiler_params=params(8),
        cost_estimate=cost(triples * rows * width * 2, triples * rows * width * 4),
        name="pack",
    )(*(pltpu.with_memory_space_constraint(y, pltpu.HBM) for y in (x, ladder, doubles)))


def fold_of(rows):
    return 5 if rows % 80 == 0 and rows < 160 else 4


def fold(x):
    q = fold_of(x.shape[0])
    m = x.shape[0] // q
    return jnp.concatenate([x[k * m : (k + 1) * m] for k in range(q)], axis=1)


def unfold(x, n):
    return jnp.concatenate([x[:, k : k + n] for k in range(0, x.shape[1], n)], axis=0)


def folded(m, n):
    q = fold_of(m)
    return jax.ShapeDtypeStruct((m // q, q * n), F32)


def product_of(x, y):
    return lax.dot_general(x, y, NT, preferred_element_type=F32)


def prepare_kernel(lam_ref, first_ref, amp_ref, keep_ref, early_ref, late_ref, all_ref, o_ref):
    pack_into(early_ref, lam_ref.at[:, LATE + FIRST :])
    pack_into(late_ref, lam_ref.at[:, :LATE])
    pack_into(all_ref, amp_ref, keep_ref)
    y = all_ref[...]
    o_ref[...] = fold(jnp.concatenate([product_of(x, y) for x in (late_ref[...], first_ref[:FIRST], early_ref[...])]))


def prepare(lam, first, amp, keep):
    triples, rows, width = lam.shape
    size = triples * width
    shapes = [
        jax.ShapeDtypeStruct((rows - LATE - FIRST, size), BF16),
        jax.ShapeDtypeStruct((LATE, size), BF16),
        jax.ShapeDtypeStruct((rows, size), BF16),
        jax.ShapeDtypeStruct((rows // 4, 4 * rows), F32),
    ]
    return pl.pallas_call(
        prepare_kernel,
        grid=(1,),
        in_specs=[whole(lam), whole(first), whole(amp), whole(keep)],
        out_specs=[whole(s) for s in shapes],
        out_shape=shapes,
        compiler_params=params(20),
        cost_estimate=cost(2 * rows * rows * size, 6 * rows * size),
        name="prepare",
    )(lam, first, amp, keep)


def gram_kernel(*refs):
    *xs, y_ref, o_ref = refs
    y = y_ref[...]
    o_ref[...] = fold(jnp.concatenate([product_of(x[: x.shape[0] // 16 * 16], y) for x in xs]))


def gram(xs, y):
    m, (n, k) = sum(x.shape[0] // 16 * 16 for x in xs), y.shape
    return pl.pallas_call(
        gram_kernel,
        in_specs=[VMEM()] * (len(xs) + 1),
        out_specs=VMEM(),
        out_shape=folded(m, n),
        compiler_params=params(8),
        cost_estimate=cost(2 * m * n * k, 2 * (m + n) * k),
        name="gram",
    )(*xs, y)


def near_kernel(step, keep_ref, lam_ref, amp_ref, cyc_ref, ladder_ref, doubles_ref, mine_ref, other_ref, o_ref, w_ref, d_ref):
    i = pl.program_id(0)
    half, width = ladder_ref.shape
    rows = lam_ref.shape[1]

    @pl.when(i == 0)
    def _():
        core, vir = core_of(), lax.axis_index("vir")
        size = half // 2 // EXTRA * width
        mine, other = mine_ref[...].astype(F32), other_ref[...].astype(F32)
        w_ref[pl.ds(pl.multiple_of(vir * half, 16), half), :] = ladder_ref[...]
        there = (1 - vir) * half
        for x, c in ((mine, core), (other, 1 - core)):
            at = pl.multiple_of(there + c * (half // 2), 16)
            w_ref[pl.ds(at, half // 2), :] = gather_back(x[:, :size], width).astype(BF16)
        own = doubles_ref[...].astype(F32)
        got = gather_back(mine[:, size : size + own.shape[0] // EXTRA * half], half)
        d_ref[:, :half] = jnp.where(vir == 0, own, got).astype(BF16)
        d_ref[:, half:] = jnp.where(vir == 0, got, own).astype(BF16)

    keep = [keep_ref[pl.ds(i * step + u, 1), :].astype(BF16) for u in range(step)]
    lam = jnp.concatenate([lam_ref[u] * keep[u] for u in range(step)], axis=0)
    mid = product_of(amp_ref[...].reshape(step * rows, width), cyc_ref[...]).astype(BF16)
    near = product_of(lam, w_ref[...]) + jnp.dot(mid, d_ref[...], preferred_element_type=F32)
    o_ref[...] = near.reshape(step, rows, width)


def near_of(lam, amp, keep, cyc, ladder, doubles, mine, other, step=4):
    triples, rows, width = lam.shape
    block = pl.BlockSpec((step, rows, width), lambda i: (i, 0, 0))
    return pl.pallas_call(
        functools.partial(near_kernel, step),
        grid=(triples // step,),
        in_specs=[whole(keep), block, block, *map(whole, (cyc, ladder, doubles, mine, other))],
        out_specs=block,
        out_shape=jax.ShapeDtypeStruct(lam.shape, F32),
        scratch_shapes=[pltpu.VMEM((width, width), BF16), pltpu.VMEM((doubles.shape[0], width), BF16)],
        compiler_params=params(12),
        cost_estimate=cost(2 * triples * rows * width * (width + 64), triples * rows * width * 8),
        name="near",
    )(keep, lam, amp, cyc, ladder, doubles, mine, other)


def add_kernel(step, norm, scale, keep_ref, lam_ref, near_ref, den_ref, o_ref):
    i = pl.program_id(0)
    den = (unfold(den_ref[...], near_ref.shape[1]) / norm).astype(BF16)
    for u in range(step):
        keep = keep_ref[pl.ds(i * step + u, 1), :] * scale
        o_ref[u] = near_ref[u] + jnp.dot(den, lam_ref[u], preferred_element_type=F32) * keep


def add_own(keep, lam, near, den, norm, scale, step=4):
    triples, rows, width = lam.shape
    block = pl.BlockSpec((step, rows, width), lambda i: (i, 0, 0))
    return pl.pallas_call(
        functools.partial(add_kernel, step, norm, scale),
        grid=(triples // step,),
        in_specs=[whole(keep), block, block, whole(den)],
        out_specs=block,
        out_shape=jax.ShapeDtypeStruct(lam.shape, F32),
        input_output_aliases={2: 0},
        compiler_params=params(12),
        cost_estimate=cost(2 * triples * rows * width * rows, triples * rows * width * 10),
        name="add_own",
    )(keep, lam, near, den)


def add_product(o_ref, near_ref, keep_ref, den, got, scale, first):
    triples, _, width = o_ref.shape
    main = width // 128 * 128
    tail = width - main
    ends_at = got.shape[1] - got.shape[1] // width * tail

    def product(lo, size):
        return jnp.dot(den, got[:, lo : lo + size], preferred_element_type=F32) * scale

    for t in range(0, triples, 2):
        ends = product(ends_at + (first + t) * tail, 2 * tail)
        for u in (t, t + 1):
            s = (u - t) * tail
            keep = keep_ref[first + u : first + u + 1, :]
            o_ref[u, :, :main] = (near_ref[u, :, :main] + product((first + u) * main, main) * keep[:, :main]).astype(BF16)
            o_ref[u, :, main:] = (near_ref[u, :, main:] + ends[:, s : s + tail] * keep[:, main:]).astype(BF16)


def early_kernel(scale, keep_ref, den_ref, *refs):
    *got, near_ref, o_ref, all_ref = refs
    at = 0
    for g in got:
        n = g.shape[0] // 16 * 16
        all_ref[at : at + n, :] = g[:n]
        at += n
    den = unfold(den_ref[...].astype(F32), at).astype(BF16)
    add_product(o_ref, near_ref, keep_ref, den, all_ref, scale, 0)


def early_output(keep, den, got, near, start, scale):
    triples, rows, width = near.shape
    spec = pl.BlockSpec((pl.Element(triples), pl.Element(rows - start), pl.Element(width)), lambda i: (0, start, 0))
    all_got = jax.ShapeDtypeStruct((rows, triples * width), BF16)
    return pl.pallas_call(
        functools.partial(early_kernel, scale),
        grid=(1,),
        in_specs=[whole(keep), whole(den), *map(whole, got), spec],
        out_specs=[spec, whole(all_got)],
        out_shape=[jax.ShapeDtypeStruct(near.shape, BF16), all_got],
        compiler_params=params(14),
        cost_estimate=cost(2 * triples * rows * width * 160, triples * rows * width * 6),
        name="early",
    )(keep, den, *got, near)


def late_kernel(scale, keep_ref, den_ref, got_ref, near_ref, _, o_ref, buf, sems):
    triples, rows, _ = buf.shape
    n = triples // PARTS
    den = unfold(den_ref[...].astype(F32), got_ref.shape[0]).astype(BF16)
    copies = []
    for k in range(PARTS):
        part = buf.at[k * n : (k + 1) * n]
        add_product(part, near_ref.at[k * n : (k + 1) * n, :rows], keep_ref, den, got_ref, scale, k * n)
        copies.append(pltpu.make_async_copy(part, o_ref.at[k * n : (k + 1) * n, :rows], sems.at[k]))
        copies[-1].start()
    for c in copies:
        c.wait()


def late_output(keep, den, got, near, out, rows, scale):
    triples, _, width = near.shape
    return pl.pallas_call(
        functools.partial(late_kernel, scale),
        in_specs=[VMEM()] * 4 + [pl.BlockSpec(memory_space=pl.ANY)],
        out_specs=pl.BlockSpec(memory_space=pl.ANY),
        out_shape=jax.ShapeDtypeStruct(near.shape, BF16),
        scratch_shapes=[pltpu.VMEM((triples, rows, width), BF16), pltpu.SemaphoreType.DMA((PARTS,))],
        input_output_aliases={4: 0},
        compiler_params=params(8),
        cost_estimate=cost(2 * triples * rows * width * 160, triples * rows * width * 6),
        name="late",
    )(keep, den, got, near, out)


def permute(x, flip, swap=0):
    n, v = lax.axis_size("occ"), lax.axis_size("vir")
    if not swap:
        return lax.ppermute(x, "occ", [(i, i ^ flip) for i in range(n)])
    return lax.ppermute(x, ("occ", "vir"), [(i * v + j, (i ^ flip) * v + (j ^ swap)) for i in range(n) for j in range(v)])


def far_sum(x):
    n = lax.axis_size("occ")
    bit = 4
    while bit < n:
        if 2 * bit < n:
            far, mid, close = permute(x, 3 * bit), permute(x, 2 * bit), permute(x, bit)
            x = (mid + far) + (close + x)
            bit *= 4
        else:
            x = x + permute(x, bit)
            bit *= 2
    return x


def near_sum(x):
    far, mid, close = permute(x, 3), permute(x, 2), permute(x, 1)
    return (x + close) + (mid + far)


def crossed(x):
    far, close = permute(x, 2, 1), permute(x, 0, 1)
    return far + close


def on_device(lam, amp, ext, ladder, cycle, doubles):
    triples, rows, width = lam.shape
    all_triples = triples * lax.axis_size("occ")
    norm = float(all_triples * width) ** 0.5
    scale = 1.0 / float(width) ** 0.5
    early_rows = rows - LATE

    ladder = ladder.T
    first_own = pack(lam, ladder, doubles, LATE)
    first_got = permute(first_own, 0, 1)
    keep = (lax.broadcasted_iota(jnp.int32, (triples, width), 1) < ext[:, None]).astype(F32)
    early_own, late_own, amp_all, own_den = prepare(lam, first_own, amp, keep)
    early_got, late_got = permute(early_own, 0, 1), permute(late_own, 0, 1)

    own_den = near_sum(own_den)
    first_got = after(first_got, own_den)
    own_den = far_sum(own_den)
    mine = first_got[FIRST:]
    other = permute(mine, 1)
    near = near_of(lam, amp, keep, cycle.T, ladder, doubles, mine, other)

    early_got = after(early_got, near)
    early = near_sum(gram((first_got, early_got), amp_all))
    near = add_own(keep, lam, near, after(own_den, early), norm, scale)

    early = far_sum(early)
    late_got = after(late_got, near)
    early = permute((early / norm).astype(BF16), 0, 1)
    late = gram((late_got,), amp_all)
    late = far_sum(late + permute(late, 1))
    early = after(early, late)
    late = (crossed(late) / norm).astype(BF16)

    got = (late_got, first_got, early_got)
    out, all_got = early_output(keep, early, got, near, LATE, scale)
    return late_output(keep, late, all_got, near, out, LATE, scale)


def solution(mesh):
    return jax.shard_map(
        on_device,
        mesh=mesh,
        in_specs=(
            P("occ", "vir", None),
            P("occ", "vir", None),
            P("occ"),
            P(None, "vir"),
            P(),
            P(None, "vir"),
        ),
        out_specs=P("occ", "vir", None),
        check_vma=False,
    )
```

```python
import functools

import jax
import jax.numpy as jnp
from jax import lax
from jax.experimental import pallas as pl
from jax.experimental.pallas import tpu as pltpu
from jax.sharding import PartitionSpec as P

F32, BF16 = jnp.float32, jnp.bfloat16
NT = (((1,), (1,)), ((), ()))
VMEM = functools.partial(pl.BlockSpec, memory_space=pltpu.VMEM)
SMEM = functools.partial(pl.BlockSpec, memory_space=pltpu.SMEM)
LATE = 64
FIRST = 48
PARTS = 4
EXTRA = 8


def params(mib, **kw):
    return pltpu.CompilerParams(vmem_limit_bytes=mib << 20, **kw)


def cost(flops, nbytes):
    return pl.CostEstimate(flops=flops, bytes_accessed=nbytes, transcendentals=0)


def whole(x):
    return pl.BlockSpec(x.shape, lambda i: (0,) * x.ndim)


def after(x, *others):
    return lax.optimization_barrier((x, *others))[0]


def pack_into(o_ref, x_ref, keep_ref=None):
    triples, _, width = x_ref.shape
    main = width // 128 * 128
    tail = width - main
    for t in range(0, triples, 2):
        pair = []
        for u in (t, t + 1):
            x = x_ref[u]
            if keep_ref is not None:
                x = x * keep_ref[u : u + 1, :].astype(BF16)
            o_ref[:, u * main : (u + 1) * main] = x[:, :main]
            pair.append(x[:, main:])
        at = triples * main + t * tail
        o_ref[:, at : at + 2 * tail] = jnp.concatenate(pair, axis=1)


def core_of():
    return lax.rem(lax.axis_index("occ"), 2)


def spread(x):
    return jnp.concatenate([x[i : i + EXTRA] for i in range(0, x.shape[0], EXTRA)], axis=1)


def gather_back(x, width):
    return jnp.concatenate([x[:, i : i + width] for i in range(0, x.shape[1], width)], axis=0)


def pack_kernel(start, x_ref, ladder_ref, doubles_ref, o_ref, x_buf, l_buf, d_buf, sems):
    triples, rows, _ = x_buf.shape
    half = ladder_ref.shape[0] // 2
    n = triples // PARTS
    first = pl.multiple_of(core_of() * half, 16)
    copies = [(x_ref.at[pl.ds(k * n, n), pl.ds(start, rows)], x_buf.at[pl.ds(k * n, n)]) for k in range(PARTS)]
    copies += [(ladder_ref.at[pl.ds(first, half)], l_buf), (doubles_ref, d_buf)]
    copies = [pltpu.make_async_copy(src, dst, sems.at[k]) for k, (src, dst) in enumerate(copies)]
    for c in copies:
        c.start()
    for c in copies:
        c.wait()
    pack_into(o_ref.at[:FIRST], x_buf)
    parts = [spread(l_buf[...].astype(F32)), spread(d_buf[...].astype(F32))]
    used = sum(p.shape[1] for p in parts)
    parts.append(jnp.zeros((EXTRA, o_ref.shape[1] - used), F32))
    o_ref[FIRST:, :] = jnp.concatenate(parts, axis=1).astype(BF16)


def pack(x, ladder, doubles, start):
    triples, rows, width = x.shape
    rows = FIRST
    return pl.pallas_call(
        functools.partial(pack_kernel, start),
        in_specs=[pl.BlockSpec(memory_space=pltpu.HBM)] * 3,
        out_specs=VMEM(),
        out_shape=jax.ShapeDtypeStruct((FIRST + EXTRA, triples * width), BF16),
        scratch_shapes=[
            pltpu.VMEM((triples, rows, width), BF16),
            pltpu.VMEM((ladder.shape[0] // 2, width), BF16),
            pltpu.VMEM(doubles.shape, BF16),
            pltpu.SemaphoreType.DMA((PARTS + 2,)),
        ],
        compiler_params=params(8),
        cost_estimate=cost(triples * rows * width * 2, triples * rows * width * 4),
        name="pack",
    )(*(pltpu.with_memory_space_constraint(y, pltpu.HBM) for y in (x, ladder, doubles)))


def fold_of(rows):
    return 5 if rows % 80 == 0 and rows < 160 else 4


def fold(x):
    q = fold_of(x.shape[0])
    m = x.shape[0] // q
    return jnp.concatenate([x[k * m : (k + 1) * m] for k in range(q)], axis=1)


def unfold(x, n):
    return jnp.concatenate([x[:, k : k + n] for k in range(0, x.shape[1], n)], axis=0)


def folded(m, n):
    q = fold_of(m)
    return jax.ShapeDtypeStruct((m // q, q * n), F32)


def product_of(x, y):
    return lax.dot_general(x, y, NT, preferred_element_type=F32)


def prepare_kernel(lam_ref, first_ref, amp_ref, keep_ref, early_ref, late_ref, all_ref, o_ref):
    pack_into(early_ref, lam_ref.at[:, LATE + FIRST :])
    pack_into(late_ref, lam_ref.at[:, :LATE])
    pack_into(all_ref, amp_ref, keep_ref)
    y = all_ref[...]
    o_ref[...] = fold(jnp.concatenate([product_of(x, y) for x in (late_ref[...], first_ref[:FIRST], early_ref[...])]))


def prepare(lam, first, amp, keep):
    triples, rows, width = lam.shape
    size = triples * width
    shapes = [
        jax.ShapeDtypeStruct((rows - LATE - FIRST, size), BF16),
        jax.ShapeDtypeStruct((LATE, size), BF16),
        jax.ShapeDtypeStruct((rows, size), BF16),
        jax.ShapeDtypeStruct((rows // 4, 4 * rows), F32),
    ]
    return pl.pallas_call(
        prepare_kernel,
        grid=(1,),
        in_specs=[whole(lam), whole(first), whole(amp), whole(keep)],
        out_specs=[whole(s) for s in shapes],
        out_shape=shapes,
        compiler_params=params(20),
        cost_estimate=cost(2 * rows * rows * size, 6 * rows * size),
        name="prepare",
    )(lam, first, amp, keep)


def gram_kernel(*refs):
    *xs, y_ref, o_ref = refs
    y = y_ref[...]
    o_ref[...] = fold(jnp.concatenate([product_of(x[: x.shape[0] // 16 * 16], y) for x in xs]))


def gram(xs, y):
    m, (n, k) = sum(x.shape[0] // 16 * 16 for x in xs), y.shape
    return pl.pallas_call(
        gram_kernel,
        in_specs=[VMEM()] * (len(xs) + 1),
        out_specs=VMEM(),
        out_shape=folded(m, n),
        compiler_params=params(8),
        cost_estimate=cost(2 * m * n * k, 2 * (m + n) * k),
        name="gram",
    )(*xs, y)


def near_kernel(step, keep_ref, lam_ref, amp_ref, cyc_ref, ladder_ref, doubles_ref, mine_ref, other_ref, o_ref, w_ref, d_ref):
    i = pl.program_id(0)
    half, width = ladder_ref.shape
    rows = lam_ref.shape[1]

    @pl.when(i == 0)
    def _():
        core, vir = core_of(), lax.axis_index("vir")
        size = half // 2 // EXTRA * width
        mine, other = mine_ref[...].astype(F32), other_ref[...].astype(F32)
        w_ref[pl.ds(pl.multiple_of(vir * half, 16), half), :] = ladder_ref[...]
        there = (1 - vir) * half
        for x, c in ((mine, core), (other, 1 - core)):
            at = pl.multiple_of(there + c * (half // 2), 16)
            w_ref[pl.ds(at, half // 2), :] = gather_back(x[:, :size], width).astype(BF16)
        own = doubles_ref[...].astype(F32)
        got = gather_back(mine[:, size : size + own.shape[0] // EXTRA * half], half)
        d_ref[:, :half] = jnp.where(vir == 0, own, got).astype(BF16)
        d_ref[:, half:] = jnp.where(vir == 0, got, own).astype(BF16)

    keep = [keep_ref[pl.ds(i * step + u, 1), :].astype(BF16) for u in range(step)]
    lam = jnp.concatenate([lam_ref[u] * keep[u] for u in range(step)], axis=0)
    mid = product_of(amp_ref[...].reshape(step * rows, width), cyc_ref[...]).astype(BF16)
    near = product_of(lam, w_ref[...]) + jnp.dot(mid, d_ref[...], preferred_element_type=F32)
    o_ref[...] = near.reshape(step, rows, width)


def near_of(lam, amp, keep, cyc, ladder, doubles, mine, other, step=4):
    triples, rows, width = lam.shape
    block = pl.BlockSpec((step, rows, width), lambda i: (i, 0, 0))
    return pl.pallas_call(
        functools.partial(near_kernel, step),
        grid=(triples // step,),
        in_specs=[whole(keep), block, block, *map(whole, (cyc, ladder, doubles, mine, other))],
        out_specs=block,
        out_shape=jax.ShapeDtypeStruct(lam.shape, F32),
        scratch_shapes=[pltpu.VMEM((width, width), BF16), pltpu.VMEM((doubles.shape[0], width), BF16)],
        compiler_params=params(12),
        cost_estimate=cost(2 * triples * rows * width * (width + 64), triples * rows * width * 8),
        name="near",
    )(keep, lam, amp, cyc, ladder, doubles, mine, other)


def add_kernel(step, norm, scale, keep_ref, lam_ref, near_ref, den_ref, o_ref):
    i = pl.program_id(0)
    den = (unfold(den_ref[...], near_ref.shape[1]) / norm).astype(BF16)
    for u in range(step):
        keep = keep_ref[pl.ds(i * step + u, 1), :] * scale
        o_ref[u] = near_ref[u] + jnp.dot(den, lam_ref[u], preferred_element_type=F32) * keep


def add_own(keep, lam, near, den, norm, scale, step=4):
    triples, rows, width = lam.shape
    block = pl.BlockSpec((step, rows, width), lambda i: (i, 0, 0))
    return pl.pallas_call(
        functools.partial(add_kernel, step, norm, scale),
        grid=(triples // step,),
        in_specs=[whole(keep), block, block, whole(den)],
        out_specs=block,
        out_shape=jax.ShapeDtypeStruct(lam.shape, F32),
        input_output_aliases={2: 0},
        compiler_params=params(12),
        cost_estimate=cost(2 * triples * rows * width * rows, triples * rows * width * 10),
        name="add_own",
    )(keep, lam, near, den)


def add_product(o_ref, near_ref, keep_ref, den, got, scale, first):
    triples, _, width = o_ref.shape
    main = width // 128 * 128
    tail = width - main
    ends_at = got.shape[1] - got.shape[1] // width * tail

    def product(lo, size):
        return jnp.dot(den, got[:, lo : lo + size], preferred_element_type=F32) * scale

    for t in range(0, triples, 2):
        ends = product(ends_at + (first + t) * tail, 2 * tail)
        for u in (t, t + 1):
            s = (u - t) * tail
            keep = keep_ref[first + u : first + u + 1, :]
            o_ref[u, :, :main] = (near_ref[u, :, :main] + product((first + u) * main, main) * keep[:, :main]).astype(BF16)
            o_ref[u, :, main:] = (near_ref[u, :, main:] + ends[:, s : s + tail] * keep[:, main:]).astype(BF16)


def early_kernel(scale, keep_ref, den_ref, *refs):
    *got, near_ref, o_ref, all_ref = refs
    at = 0
    for g in got:
        n = g.shape[0] // 16 * 16
        all_ref[at : at + n, :] = g[:n]
        at += n
    den = unfold(den_ref[...].astype(F32), at).astype(BF16)
    add_product(o_ref, near_ref, keep_ref, den, all_ref, scale, 0)


def early_output(keep, den, got, near, start, scale):
    triples, rows, width = near.shape
    spec = pl.BlockSpec((pl.Element(triples), pl.Element(rows - start), pl.Element(width)), lambda i: (0, start, 0))
    all_got = jax.ShapeDtypeStruct((rows, triples * width), BF16)
    return pl.pallas_call(
        functools.partial(early_kernel, scale),
        grid=(1,),
        in_specs=[whole(keep), whole(den), *map(whole, got), spec],
        out_specs=[spec, whole(all_got)],
        out_shape=[jax.ShapeDtypeStruct(near.shape, BF16), all_got],
        compiler_params=params(14),
        cost_estimate=cost(2 * triples * rows * width * 160, triples * rows * width * 6),
        name="early",
    )(keep, den, *got, near)


def late_kernel(scale, keep_ref, den_ref, got_ref, near_ref, _, o_ref, buf, sems):
    triples, rows, _ = buf.shape
    n = triples // PARTS
    den = unfold(den_ref[...].astype(F32), got_ref.shape[0]).astype(BF16)
    copies = []
    for k in range(PARTS):
        part = buf.at[k * n : (k + 1) * n]
        add_product(part, near_ref.at[k * n : (k + 1) * n, :rows], keep_ref, den, got_ref, scale, k * n)
        copies.append(pltpu.make_async_copy(part, o_ref.at[k * n : (k + 1) * n, :rows], sems.at[k]))
        copies[-1].start()
    for c in copies:
        c.wait()


def late_output(keep, den, got, near, out, rows, scale):
    triples, _, width = near.shape
    return pl.pallas_call(
        functools.partial(late_kernel, scale),
        in_specs=[VMEM()] * 4 + [pl.BlockSpec(memory_space=pl.ANY)],
        out_specs=pl.BlockSpec(memory_space=pl.ANY),
        out_shape=jax.ShapeDtypeStruct(near.shape, BF16),
        scratch_shapes=[pltpu.VMEM((triples, rows, width), BF16), pltpu.SemaphoreType.DMA((PARTS,))],
        input_output_aliases={4: 0},
        compiler_params=params(8),
        cost_estimate=cost(2 * triples * rows * width * 160, triples * rows * width * 6),
        name="late",
    )(keep, den, got, near, out)


def permute(x, flip, swap=0):
    n, v = lax.axis_size("occ"), lax.axis_size("vir")
    if not swap:
        return lax.ppermute(x, "occ", [(i, i ^ flip) for i in range(n)])
    return lax.ppermute(x, ("occ", "vir"), [(i * v + j, (i ^ flip) * v + (j ^ swap)) for i in range(n) for j in range(v)])


def far_sum(x):
    n = lax.axis_size("occ")
    bit = 4
    while bit < n:
        if 2 * bit < n:
            far, mid, close = permute(x, 3 * bit), permute(x, 2 * bit), permute(x, bit)
            x = (mid + far) + (close + x)
            bit *= 4
        else:
            x = x + permute(x, bit)
            bit *= 2
    return x


def two_step_sum(x):
    x = x + permute(x, 1)
    return x + permute(x, 2)


def near_sum(x):
    far, mid, close = permute(x, 3), permute(x, 2), permute(x, 1)
    return (x + close) + (mid + far)


def crossed(x):
    far, close = permute(x, 2, 1), permute(x, 0, 1)
    return far + close


def on_device(lam, amp, ext, ladder, cycle, doubles):
    triples, rows, width = lam.shape
    all_triples = triples * lax.axis_size("occ")
    norm = float(all_triples * width) ** 0.5
    scale = 1.0 / float(width) ** 0.5
    early_rows = rows - LATE

    ladder = ladder.T
    first_own = pack(lam, ladder, doubles, LATE)
    first_got = permute(first_own, 0, 1)
    keep = (lax.broadcasted_iota(jnp.int32, (triples, width), 1) < ext[:, None]).astype(F32)
    early_own, late_own, amp_all, own_den = prepare(lam, first_own, amp, keep)
    early_got, late_got = permute(early_own, 0, 1), permute(late_own, 0, 1)

    own_den = near_sum(own_den)
    first_got = after(first_got, own_den)
    own_den = far_sum(own_den)
    mine = first_got[FIRST:]
    other = permute(mine, 1)
    near = near_of(lam, amp, keep, cycle.T, ladder, doubles, mine, other)

    early_got = after(early_got, near)
    early = two_step_sum(gram((first_got, early_got), amp_all))
    near = add_own(keep, lam, near, after(own_den, early), norm, scale)

    early = far_sum(early)
    late_got = after(late_got, near)
    early = permute((early / norm).astype(BF16), 0, 1)
    late = gram((late_got,), amp_all)
    late = far_sum(late + permute(late, 1))
    early = after(early, late)
    late = (crossed(late) / norm).astype(BF16)

    got = (late_got, first_got, early_got)
    out, all_got = early_output(keep, early, got, near, LATE, scale)
    return late_output(keep, late, all_got, near, out, LATE, scale)


def solution(mesh):
    return jax.shard_map(
        on_device,
        mesh=mesh,
        in_specs=(
            P("occ", "vir", None),
            P("occ", "vir", None),
            P("occ"),
            P(None, "vir"),
            P(),
            P(None, "vir"),
        ),
        out_specs=P("occ", "vir", None),
        check_vma=False,
    )
```
